512 devices in a mesh: wide: 64 (over y, x, core), narrow: 8 (over z).
Axes of the slice: x: 4, y: 8, z: 8, core: 2. Of those that a mesh axis runs over, the one named last changes fastest.
Arguments:
- effects_start: float32 [262144, 256], P(('wide', 'narrow')), may hold values from -3 to 3
- marginal: float32 [262144, 256], P(('wide', 'narrow')), may hold values from -6 to 6
- ld_diag: float32 [262144, 512], P(('wide', 'narrow')), may hold values from -1 to 1, as said below
- ld_upper: float32 [262144, 512], P(('wide', 'narrow')), may hold values from -1 to 1
- penalty_grid: float32 [16], replicated, may hold values from 0.1 to 1
- penalty_index: int32 [256], replicated, may hold values from 0 to 15
- dosages: bfloat16 [1024, 262144], P(None, ('wide', 'narrow')), may hold values from 0 to 2
- stack_weights: float32 [256, 256], replicated, may hold values from -0.375 to 0.375
Outputs:
- effects: float32 [262144, 256], P(('wide', 'narrow'))
- stacked: float32 [1024, 256], P(('wide', 'narrow'))
The draws below stay inside these ranges and needn't reach their ends.
Inputs may be any that keep to these rules, and one draw needn't show every extreme that they name: `ld_diag`: each diagonal tile is symmetric.
All inputs are finite; a program needn't handle non-finite values.
Results may differ from the reference program's by a relative error of at most 0.0037.
Values sent between devices are 32-bit elements; how exact they have to be, the bound alone decides.
No kernel may reach another device: no remote copies, remote signals or barrier semaphores. Data moves between devices by JAX's collectives and lax.ppermute only.
A program may use at most 64 MiB of HBM per device.

```python
import math
import jax
import jax.numpy as jnp
from jax import lax

VAR_DEV = 512
K = 256
LEVELS = 16
ITERS = 3
M = 262144
N_IND = 1024


def tile_entries(key):
    strips = M // VAR_DEV
    raw = jnp.clip(jax.random.normal(key, (strips, VAR_DEV, VAR_DEV), jnp.float32), -4.0, 4.0)
    return raw * (0.25 / math.sqrt(VAR_DEV))


def draw_ld_diag(key, part):
    raw = tile_entries(jax.random.fold_in(key, 11))
    symmetric = (raw + jnp.swapaxes(raw, 1, 2)) / math.sqrt(2.0)
    identity = jnp.eye(VAR_DEV, dtype=jnp.float32)
    tiles = symmetric * (1.0 - identity)[None] + identity[None]
    return tiles.reshape(M, VAR_DEV)


def draw_ld_upper(key, part):
    raw = tile_entries(jax.random.fold_in(key, 23))
    return raw.reshape(M, VAR_DEV)


def with_ends(array, stream_key, least, high):
    shape = array.shape
    index_at = [jax.random.randint(jax.random.fold_in(stream_key, axis), (), 0, shape[axis]) for axis in range(len(shape))]
    array = array.at[tuple(index_at)].set(least)
    longest = shape.index(max(shape))
    index_at[longest] = (index_at[longest] + 1) % shape[longest]
    return array.at[tuple(index_at)].set(high)


def level_of(own_key, dims, pieces, low, largest):
    loudness = 1.0
    for axis_at, parts in pieces:
        heights = jax.random.uniform(jax.random.fold_in(jax.random.fold_in(own_key, 6), axis_at), (parts,), jnp.float32, low / len(pieces), largest / len(pieces))
        loudness = loudness * jnp.repeat(jnp.exp(heights), dims[axis_at] // parts).reshape((-1,) + (1,) * (len(dims) - 1 - axis_at))
    return loudness


def centred(stream_key, dims, spread, bound, shards=(), held_as=jnp.bfloat16):
    drawn = jax.random.normal(stream_key, dims, jnp.float32) * spread
    if len(shards) > 0:
        drawn = level_of(stream_key, dims, shards, -0.22, 0.18) * drawn
    return jnp.clip(drawn, min=-bound, max=bound).astype(held_as)


def setup_inputs(seed: int = 0) -> dict:
    seeds = jax.random.split(jax.random.key(seed), 9)
    effects_start = centred(seeds[0], (M, K), 0.5, 3.0, ((0, 512),), jnp.float32)
    marginal = centred(seeds[1], (M, K), 1.0, 6.0, ((0, 512),), jnp.float32)
    ld_diag = draw_ld_diag(jax.random.fold_in(seeds[8], 71), 0)
    ld_upper = draw_ld_upper(jax.random.fold_in(seeds[8], 71), 0)
    penalty_grid = jnp.clip(jnp.exp(jax.random.uniform(seeds[4], (LEVELS,), jnp.float32, math.log(0.1), math.log(1.0))), 0.1, 1.0)
    penalty_index = with_ends(jax.random.randint(seeds[5], (K,), 0, LEVELS), jax.random.fold_in(seeds[5], 1), 0, LEVELS - 1).astype(jnp.int32)
    dosages = jnp.clip(2.0 * jax.random.uniform(seeds[6], (N_IND, M), jnp.float32) ** level_of(seeds[6], (N_IND, M), ((1, 512),), -0.2, 0.2), 0.0, 2.0).astype(jnp.bfloat16)
    stack_weights = centred(seeds[7], (K, K), K ** -0.5, 0.375, (), jnp.float32)
    return dict(effects_start=effects_start, marginal=marginal, ld_diag=ld_diag, ld_upper=ld_upper, penalty_grid=penalty_grid, penalty_index=penalty_index, dosages=dosages, stack_weights=stack_weights)


step_size = 0.5

def reference(effects_start, marginal, ld_diag, ld_upper, penalty_grid, penalty_index, dosages, stack_weights):
    strips = M // VAR_DEV
    diag_blocks = ld_diag.reshape(strips, VAR_DEV, VAR_DEV)
    upper_blocks = ld_upper.reshape(strips, VAR_DEV, VAR_DEV)
    threshold = step_size * penalty_grid[penalty_index]
    effects = effects_start
    for sweep in range(ITERS):
        blocked = effects.reshape(strips, VAR_DEV, K)
        product = jnp.einsum('sij,sjk->sik', diag_blocks, blocked, precision=lax.Precision.HIGHEST)
        ahead = jnp.einsum('sij,sjk->sik', upper_blocks[:-1], blocked[1:], precision=lax.Precision.HIGHEST)
        behind = jnp.einsum('sji,sjk->sik', upper_blocks[:-1], blocked[:-1], precision=lax.Precision.HIGHEST)
        zero_block = jnp.zeros((1, VAR_DEV, K), jnp.float32)
        product = product + jnp.concatenate([ahead, zero_block], axis=0) + jnp.concatenate([zero_block, behind], axis=0)
        gradient = product.reshape(M, K) - marginal
        moved = effects - step_size * gradient
        effects = jnp.sign(moved) * jnp.maximum(jnp.abs(moved) - threshold[None, :], 0.0)
    effects_low = effects.astype(jnp.bfloat16)
    shrink = 1.0 / math.sqrt(M)
    scores = jnp.dot(dosages, effects_low, preferred_element_type=jnp.float32) * shrink
    stacked = jnp.dot(scores, stack_weights, precision=lax.Precision.HIGHEST, preferred_element_type=jnp.float32)
    return (effects, stacked)
```

```python
import math

import jax
import jax.numpy as jnp
from jax import lax
from jax.sharding import Mesh, PartitionSpec as P

ITERS = 3
SPLIT = (("y", 8), ("x", 4), ("c", 2), ("z", 8))
ALL = tuple(name for name, _ in SPLIT)
STAGES = (("y", "x", "z"),)
PREC = lax.Precision.HIGH

step_size = 0.5


def passed_along(block, distance):
    count = lax.axis_size(ALL)
    route = [(i - distance, i) for i in range(count) if 0 <= i - distance < count]
    return lax.ppermute(block, ALL, route)


def dot(left, right):
    return jnp.dot(left, right, precision=PREC, preferred_element_type=jnp.float32)


def transposed_dot(left, right):
    return lax.dot_general(
        left, right, (((0,), (0,)), ((), ())), precision=PREC, preferred_element_type=jnp.float32
    )


def exchange_sum(block, axes):
    count = lax.axis_size(axes)
    rows = block.shape[0] // count
    got = lax.all_to_all(block.reshape(count, rows, block.shape[1]), axes, 0, 0, tiled=True)
    return jnp.sum(got, axis=0)


def shards(
    effects_start, marginal, ld_diag, ld_upper, penalty_grid, penalty_index, dosages, stack_weights
):
    variants = ld_diag.shape[0]
    levels = penalty_grid.shape[0]
    individuals = dosages.shape[0]
    picked = (penalty_index[None, :] == jnp.arange(levels, dtype=jnp.int32)[:, None]).astype(
        jnp.float32
    )
    threshold = step_size * jnp.sum(picked * penalty_grid[:, None], axis=0)

    core = lax.axis_index("c")
    lines = lax.axis_size(("y", "x"))
    by_core = dosages.reshape(lines, 2, individuals // (2 * lines), variants)

    def half(which):
        part = lax.dynamic_index_in_dim(by_core, which, axis=1, keepdims=False)
        return part.reshape(individuals // 2, variants)

    dosages_mine, dosages_other = half(core), half(1 - core)

    effects = effects_start
    for sweep in range(ITERS):
        ahead = passed_along(effects, -1)
        behind = passed_along(transposed_dot(ld_upper, effects), 1)
        gradient = dot(ld_diag, effects) + dot(ld_upper, ahead) + behind - marginal
        moved = effects - step_size * gradient
        effects = jnp.sign(moved) * jnp.maximum(jnp.abs(moved) - threshold[None, :], 0.0)

    low = effects.astype(jnp.bfloat16)
    other = jnp.dot(dosages_other, low, preferred_element_type=jnp.float32)
    got = lax.ppermute(other, "c", [(0, 1), (1, 0)])
    summed = jnp.dot(dosages_mine, low, preferred_element_type=jnp.float32) + got
    for axes in STAGES:
        summed = exchange_sum(summed, axes)
    shrink = 1.0 / math.sqrt(variants * lax.axis_size(ALL))
    scores = summed * shrink
    stacked = jnp.dot(
        scores, stack_weights, precision=lax.Precision.HIGHEST, preferred_element_type=jnp.float32
    )
    return (effects, stacked)


def solution(mesh):
    fine = Mesh(mesh.devices.reshape([size for _, size in SPLIT]), ALL)
    return jax.shard_map(
        shards,
        mesh=fine,
        in_specs=(
            P(ALL, None),
            P(ALL, None),
            P(ALL, None),
            P(ALL, None),
            P(),
            P(),
            P(None, ALL),
            P(),
        ),
        out_specs=(P(ALL, None), P(ALL, None)),
        check_vma=False,
    )
```

```python
import math

import jax
import jax.numpy as jnp
from jax import lax
from jax.sharding import Mesh, PartitionSpec as P

ITERS = 3
SPLIT = (("yh", 4), ("yl", 2), ("x", 4), ("c", 2), ("z", 8))
ALL = tuple(name for name, _ in SPLIT)
STAGES = (("yl", "x"), ("yh", "z"))
PREC = lax.Precision.HIGH

step_size = 0.5


def passed_along(block, distance):
    count = lax.axis_size(ALL)
    route = [(i - distance, i) for i in range(count) if 0 <= i - distance < count]
    return lax.ppermute(block, ALL, route)


def dot(left, right):
    return jnp.dot(left, right, precision=PREC, preferred_element_type=jnp.float32)


def transposed_dot(left, right):
    return lax.dot_general(
        left, right, (((0,), (0,)), ((), ())), precision=PREC, preferred_element_type=jnp.float32
    )


def exchange_sum(block, axes):
    count = lax.axis_size(axes)
    rows = block.shape[0] // count
    got = lax.all_to_all(block.reshape(count, rows, block.shape[1]), axes, 0, 0, tiled=True)
    return jnp.sum(got, axis=0)


def shards(
    effects_start, marginal, ld_diag, ld_upper, penalty_grid, penalty_index, dosages, stack_weights
):
    variants = ld_diag.shape[0]
    levels = penalty_grid.shape[0]
    individuals = dosages.shape[0]
    picked = (penalty_index[None, :] == jnp.arange(levels, dtype=jnp.int32)[:, None]).astype(
        jnp.float32
    )
    threshold = step_size * jnp.sum(picked * penalty_grid[:, None], axis=0)

    core = lax.axis_index("c")
    outer = [size for _, size in SPLIT[:4]]
    by_core = dosages.reshape(*outer, individuals // math.prod(outer), variants)

    def half(which):
        part = lax.dynamic_index_in_dim(by_core, which, axis=3, keepdims=False)
        return part.transpose(1, 2, 0, 3, 4).reshape(individuals // 2, variants)

    dosages_mine, dosages_other = half(core), half(1 - core)

    effects = effects_start
    for _ in range(ITERS):
        ahead = passed_along(effects, -1)
        handed = transposed_dot(ld_upper, effects)
        behind = passed_along(handed, 1)
        own = dot(ld_diag, effects)
        known = own + dot(ld_upper, ahead) - marginal
        known = lax.optimization_barrier(known)
        moved = effects - step_size * (known + behind)
        effects = jnp.sign(moved) * jnp.maximum(jnp.abs(moved) - threshold[None, :], 0.0)

    low = effects.astype(jnp.bfloat16)
    other = jnp.dot(dosages_other, low, preferred_element_type=jnp.float32)
    got = lax.ppermute(other, "c", [(0, 1), (1, 0)])
    summed = jnp.dot(dosages_mine, low, preferred_element_type=jnp.float32) + got
    for axes in STAGES:
        summed = exchange_sum(summed, axes)
    shrink = 1.0 / math.sqrt(variants * lax.axis_size(ALL))
    scores = summed * shrink
    stacked = jnp.dot(
        scores, stack_weights, precision=PREC, preferred_element_type=jnp.float32
    )
    return (effects, stacked)


def solution(mesh):
    fine = Mesh(mesh.devices.reshape([size for _, size in SPLIT]), ALL)
    return jax.shard_map(
        shards,
        mesh=fine,
        in_specs=(
            P(ALL, None),
            P(ALL, None),
            P(ALL, None),
            P(ALL, None),
            P(),
            P(),
            P(None, ALL),
            P(),
        ),
        out_specs=(P(ALL, None), P(ALL, None)),
        check_vma=False,
    )
```

```python
import math

import jax
import jax.numpy as jnp
from jax import lax
from jax.experimental import pallas as pl
from jax.experimental.pallas import tpu as pltpu
from jax.sharding import Mesh, PartitionSpec as P

ITERS = 3
SPLIT = (("yh", 4), ("yl", 2), ("x", 4), ("c", 2), ("z", 8))
ALL = tuple(name for name, _ in SPLIT)
STAGES = (("yl", "x"), ("yh", "z"))
PREC = lax.Precision.HIGH

step_size = 0.5


def passed_along(block, distance):
    count = lax.axis_size(ALL)
    route = [(i - distance, i) for i in range(count) if 0 <= i - distance < count]
    return lax.ppermute(block, ALL, route)


def dot(left, right):
    return jnp.dot(left, right, precision=PREC, preferred_element_type=jnp.float32)


def transposed_dot(left, right):
    return lax.dot_general(
        left, right, (((0,), (0,)), ((), ())), precision=PREC, preferred_element_type=jnp.float32
    )


def exchange_sum(block, axes):
    count = lax.axis_size(axes)
    rows = block.shape[0] // count
    got = lax.all_to_all(block.reshape(count, rows, block.shape[1]), axes, 0, 0, tiled=True)
    return jnp.sum(got, axis=0)


def turn_rows(rows_ref, mine_ref, other_ref, arrived):
    core = lax.axis_index("c")
    copies = []
    for half, out_ref in enumerate((mine_ref, other_ref)):
        which = lax.rem(core + half, 2)
        for j in range(out_ref.shape[0]):
            for k in range(out_ref.shape[1]):
                copies.append(
                    pltpu.make_async_copy(
                        rows_ref.at[:, j, k, which], out_ref.at[j, k], arrived.at[len(copies)]
                    )
                )
    for copy in copies:
        copy.start()
    for copy in copies:
        copy.wait()


def pick(by_core):
    yh, yl, x, _, rows, variants = by_core.shape
    half = jax.ShapeDtypeStruct((yl, x, yh, rows, variants), by_core.dtype)
    return pl.pallas_call(
        turn_rows,
        in_specs=[pl.BlockSpec(memory_space=pltpu.HBM)],
        out_specs=[pl.BlockSpec(memory_space=pltpu.VMEM)] * 2,
        out_shape=[half, half],
        scratch_shapes=[pltpu.SemaphoreType.DMA((2 * yl * x,))],
        compiler_params=pltpu.CompilerParams(vmem_limit_bytes=4 * 1024 * 1024),
        cost_estimate=pl.CostEstimate(
            flops=0, bytes_accessed=4 * by_core.size, transcendentals=0
        ),
        name="pick",
    )(by_core)


def shards(
    effects_start, marginal, ld_diag, ld_upper, penalty_grid, penalty_index, dosages, stack_weights
):
    variants = ld_diag.shape[0]
    levels = penalty_grid.shape[0]
    individuals = dosages.shape[0]
    picked = (penalty_index[None, :] == jnp.arange(levels, dtype=jnp.int32)[:, None]).astype(
        jnp.float32
    )
    threshold = step_size * jnp.sum(picked * penalty_grid[:, None], axis=0)

    outer = [size for _, size in SPLIT[:4]]
    by_core = dosages.reshape(*outer, individuals // math.prod(outer), variants)

    halves = pick(by_core)
    dosages_mine, dosages_other = [part.reshape(individuals // 2, variants) for part in halves]

    effects = effects_start
    for _ in range(ITERS):
        ahead = passed_along(effects, -1)
        handed = transposed_dot(ld_upper, effects)
        behind = passed_along(handed, 1)
        own = dot(ld_diag, effects)
        known = own + dot(ld_upper, ahead) - marginal
        known = lax.optimization_barrier(known)
        moved = effects - step_size * (known + behind)
        effects = jnp.sign(moved) * jnp.maximum(jnp.abs(moved) - threshold[None, :], 0.0)

    low = effects.astype(jnp.bfloat16)
    other = jnp.dot(dosages_other, low, preferred_element_type=jnp.float32)
    got = lax.ppermute(other, "c", [(0, 1), (1, 0)])
    summed = jnp.dot(dosages_mine, low, preferred_element_type=jnp.float32) + got
    for axes in STAGES:
        summed = exchange_sum(summed, axes)
    shrink = 1.0 / math.sqrt(variants * lax.axis_size(ALL))
    scores = summed * shrink
    stacked = jnp.dot(
        scores, stack_weights, precision=PREC, preferred_element_type=jnp.float32
    )
    return (effects, stacked)


def solution(mesh):
    fine = Mesh(mesh.devices.reshape([size for _, size in SPLIT]), ALL)
    return jax.shard_map(
        shards,
        mesh=fine,
        in_specs=(
            P(ALL, None),
            P(ALL, None),
            P(ALL, None),
            P(ALL, None),
            P(),
            P(),
            P(None, ALL),
            P(),
        ),
        out_specs=(P(ALL, None), P(ALL, None)),
        check_vma=False,
    )
```

```python
import math

import jax
import jax.numpy as jnp
from jax import lax
from jax.experimental import pallas as pl
from jax.experimental.pallas import tpu as pltpu
from jax.sharding import Mesh, PartitionSpec as P

ITERS = 3
SPLIT = (("yh", 4), ("yl", 2), ("x", 4), ("c", 2), ("z", 8))
ALL = tuple(name for name, _ in SPLIT)
STAGES = (("yl", "x"), ("yh", "z"))
PREC = lax.Precision.HIGH

step_size = 0.5


def passed_along(block, distance):
    count = lax.axis_size(ALL)
    route = [(i - distance, i) for i in range(count) if 0 <= i - distance < count]
    return lax.ppermute(block, ALL, route)


def dot(left, right):
    return jnp.dot(left, right, precision=PREC, preferred_element_type=jnp.float32)


def transposed_dot(left, right):
    return lax.dot_general(
        left, right, (((0,), (0,)), ((), ())), precision=PREC, preferred_element_type=jnp.float32
    )


def exchange_sum(block, axes):
    count = lax.axis_size(axes)
    rows = block.shape[0] // count
    got = lax.all_to_all(block.reshape(count, rows, block.shape[1]), axes, 0, 0, tiled=True)
    return jnp.sum(got, axis=0)


def turn_rows(rows_ref, mine_ref, other_ref, arrived):
    core = lax.axis_index("c")
    copies = []
    for half, out_ref in enumerate((mine_ref, other_ref)):
        which = lax.rem(core + half, 2)
        for j in range(out_ref.shape[0]):
            for k in range(out_ref.shape[1]):
                copies.append(
                    pltpu.make_async_copy(
                        rows_ref.at[:, j, k, which], out_ref.at[j, k], arrived.at[len(copies)]
                    )
                )
    for copy in copies:
        copy.start()
    for copy in copies:
        copy.wait()


def bring_block(block_ref, out_ref, arrived):
    copy = pltpu.make_async_copy(block_ref, out_ref, arrived)
    copy.start()
    copy.wait()


def bring(block):
    return pl.pallas_call(
        bring_block,
        in_specs=[pl.BlockSpec(memory_space=pltpu.HBM)],
        out_specs=pl.BlockSpec(memory_space=pltpu.VMEM),
        out_shape=jax.ShapeDtypeStruct(block.shape, block.dtype),
        scratch_shapes=[pltpu.SemaphoreType.DMA],
        compiler_params=pltpu.CompilerParams(vmem_limit_bytes=4 * 1024 * 1024),
        cost_estimate=pl.CostEstimate(flops=0, bytes_accessed=8 * block.size, transcendentals=0),
        name="bring",
    )(block)


def pick(by_core):
    yh, yl, x, _, rows, variants = by_core.shape
    half = jax.ShapeDtypeStruct((yl, x, yh, rows, variants), by_core.dtype)
    return pl.pallas_call(
        turn_rows,
        in_specs=[pl.BlockSpec(memory_space=pltpu.HBM)],
        out_specs=[pl.BlockSpec(memory_space=pltpu.VMEM)] * 2,
        out_shape=[half, half],
        scratch_shapes=[pltpu.SemaphoreType.DMA((2 * yl * x,))],
        compiler_params=pltpu.CompilerParams(vmem_limit_bytes=4 * 1024 * 1024),
        cost_estimate=pl.CostEstimate(
            flops=0, bytes_accessed=4 * by_core.size, transcendentals=0
        ),
        name="pick",
    )(by_core)


def shards(
    effects_start, marginal, ld_diag, ld_upper, penalty_grid, penalty_index, dosages, stack_weights
):
    variants = ld_diag.shape[0]
    levels = penalty_grid.shape[0]
    individuals = dosages.shape[0]
    picked = (penalty_index[None, :] == jnp.arange(levels, dtype=jnp.int32)[:, None]).astype(
        jnp.float32
    )
    threshold = step_size * jnp.sum(picked * penalty_grid[:, None], axis=0)

    outer = [size for _, size in SPLIT[:4]]
    by_core = dosages.reshape(*outer, individuals // math.prod(outer), variants)

    halves = pick(by_core)
    dosages_mine, dosages_other = [part.reshape(individuals // 2, variants) for part in halves]

    stack_weights = bring(stack_weights)
    effects = effects_start
    for _ in range(ITERS):
        ahead = passed_along(effects, -1)
        handed = transposed_dot(ld_upper, effects)
        behind = passed_along(handed, 1)
        own = dot(ld_diag, effects)
        known = own + dot(ld_upper, ahead) - marginal
        known = lax.optimization_barrier(known)
        moved = effects - step_size * (known + behind)
        effects = jnp.sign(moved) * jnp.maximum(jnp.abs(moved) - threshold[None, :], 0.0)

    low = effects.astype(jnp.bfloat16)
    other = jnp.dot(dosages_other, low, preferred_element_type=jnp.float32)
    got = lax.ppermute(other, "c", [(0, 1), (1, 0)])
    summed = jnp.dot(dosages_mine, low, preferred_element_type=jnp.float32) + got
    shrink = 1.0 / math.sqrt(variants * lax.axis_size(ALL))
    scores = exchange_sum(summed, STAGES[0]) * shrink
    stacked = exchange_sum(dot(scores, stack_weights), STAGES[1])
    return (effects, stacked)


def solution(mesh):
    fine = Mesh(mesh.devices.reshape([size for _, size in SPLIT]), ALL)
    return jax.shard_map(
        shards,
        mesh=fine,
        in_specs=(
            P(ALL, None),
            P(ALL, None),
            P(ALL, None),
            P(ALL, None),
            P(),
            P(),
            P(None, ALL),
            P(),
        ),
        out_specs=(P(ALL, None), P(ALL, None)),
        check_vma=False,
    )
```
